32 devices in a mesh: ctx: 8 (over y, x, core), ch: 4 (over z).
Axes of the slice: x: 2, y: 2, z: 4, core: 2. Of those that a mesh axis runs over, the one named last changes fastest.
Arguments:
- query_act: bfloat16 [4096, 4096], P('ctx', 'ch'), may hold values from -6 to 6
- key_act: bfloat16 [4096, 4096], P('ctx', 'ch'), may hold values from -6 to 6
- value_act: bfloat16 [4096, 4096], P('ctx', 'ch'), may hold values from -6 to 6
- filters: bfloat16 [4096, 128], P('ch'), may hold values from -0.5 to 0.5
- proj_weight: bfloat16 [8192, 4096], P('ctx', 'ch'), may hold values from -0.09375 to 0.09375
- cotangent: bfloat16 [4096, 8192], P('ctx', 'ch'), may hold values from -6 to 6
Outputs:
- grad_query: bfloat16 [4096, 4096], P('ctx', 'ch')
- grad_key: bfloat16 [4096, 4096], P('ctx', 'ch')
- grad_value: bfloat16 [4096, 4096], P('ctx', 'ch')
- grad_filter: float32 [4096, 128], P('ch')
- grad_proj: float32 [8192, 4096], P('ctx', 'ch')
The draws below stay inside these ranges and needn't reach their ends.
All inputs are finite; a program needn't handle non-finite values.
Results may differ from the reference program's by a relative error of at most 0.0051.
Values may be sent and summed in bfloat16 or wider, within the bound.
A program may use at most 192 MiB of HBM per device.

```python
import jax
import jax.numpy as jnp
from jax import lax

D = 8192
C = 4096
TAPS = 128
TOKENS = 4096


def strengthened(array, own_key, source, target, shards_of, factor):
    owner, partner = [(jnp.arange(array.shape[axis_at]) // (array.shape[axis_at] // shards_of)).reshape([-1 if axis == axis_at else 1 for axis in range(array.ndim)]) for axis_at in (source, target)]
    chosen = jax.random.permutation(own_key, shards_of)[partner]
    strong = (owner == chosen) | (owner == (partner + shards_of // 2) % shards_of)
    return jnp.where(strong, factor * array, array)


def level_of(stream_key, extent, split, smallest, top_value):
    loudness = 1.0
    for axis_at, blocks in split:
        draws = jax.random.uniform(jax.random.fold_in(jax.random.fold_in(stream_key, 6), axis_at), (blocks,), jnp.float32, smallest / len(split), top_value / len(split))
        loudness = loudness * jnp.repeat(jnp.exp(draws), extent[axis_at] // blocks).reshape((-1,) + (1,) * (len(extent) - 1 - axis_at))
    return loudness


def bell_draw(stream_key, extent, width, most, shards=(), held_as=jnp.bfloat16):
    gain = level_of(stream_key, extent, shards, -0.22, 0.18) if shards else 1.0
    result = jax.random.normal(stream_key, extent, jnp.float32) * width * gain
    return jnp.minimum(jnp.maximum(result, -most), most).astype(held_as)


def bell_draw_with(key, dims, scale, reach, pieces, heavy, held_as=jnp.bfloat16):
    values = scale * jax.random.normal(key, dims, jnp.float32)
    if pieces:
        values = values * level_of(key, dims, pieces, -0.22, 0.18)
    return jnp.clip(strengthened(values, jax.random.fold_in(key, 3), *heavy), -reach, reach).astype(held_as)


def setup_inputs(seed: int = 0) -> dict:
    keys = jax.random.split(jax.random.key(seed), 7)
    return {
        "query_act": bell_draw(keys[0], (TOKENS, C), 1.0, 6.0, ((0, 8), (1, 4))),
        "key_act": bell_draw(keys[1], (TOKENS, C), 1.0, 6.0, ((0, 8), (1, 4))),
        "value_act": bell_draw(keys[2], (TOKENS, C), 1.0, 6.0, ((0, 8), (1, 4))),
        "filters": bell_draw(keys[3], (C, TAPS), TAPS ** -0.5, 0.5, ((0, 4),)),
        "proj_weight": bell_draw(keys[4], (D, C), C ** -0.5, 0.09375, ((0, 8), (1, 4))),
        "cotangent": bell_draw_with(keys[5], (TOKENS, D), 1.0, 6.0, ((0, 8), (1, 4)), (0, 1, 8, 2.0)),
    }


def causal_mix(filt, signal):
    padded = jnp.concatenate([jnp.zeros((TAPS - 1, signal.shape[1]), jnp.float32), signal], 0)

    def add_tap(lag_index, total):
        offset = jnp.int32(TAPS - 1) - lag_index.astype(jnp.int32)
        portion = lax.dynamic_slice_in_dim(padded, offset, signal.shape[0], 0)
        column = lax.dynamic_index_in_dim(filt, lag_index.astype(jnp.int32), 1, keepdims=False)
        return total + column[None, :] * portion

    return lax.fori_loop(0, TAPS, add_tap, jnp.zeros(signal.shape, jnp.float32))


def anti_mix(filt, signal):
    padded = jnp.concatenate([signal, jnp.zeros((TAPS - 1, signal.shape[1]), jnp.float32)], 0)

    def add_tap(lag_index, total):
        offset = lag_index.astype(jnp.int32)
        portion = lax.dynamic_slice_in_dim(padded, offset, signal.shape[0], 0)
        column = lax.dynamic_index_in_dim(filt, lag_index.astype(jnp.int32), 1, keepdims=False)
        return total + column[None, :] * portion

    return lax.fori_loop(0, TAPS, add_tap, jnp.zeros(signal.shape, jnp.float32))


def filter_terms(grad_gate, product):
    padded = jnp.concatenate([jnp.zeros((TAPS - 1, product.shape[1]), jnp.float32), product], 0)

    def one_lag(lag_index):
        offset = jnp.int32(TAPS - 1) - lag_index.astype(jnp.int32)
        portion = lax.dynamic_slice_in_dim(padded, offset, product.shape[0], 0)
        return jnp.sum(grad_gate * portion, axis=0)

    return lax.map(one_lag, jnp.arange(TAPS, dtype=jnp.int32)).T


def reference(query_act, key_act, value_act, filters, proj_weight, cotangent):
    query_f = query_act.astype(jnp.float32)
    key_f = key_act.astype(jnp.float32)
    value_f = value_act.astype(jnp.float32)
    filt = filters.astype(jnp.float32)
    product = (key_f * value_f).astype(jnp.bfloat16)
    product_f = product.astype(jnp.float32)
    mixed = causal_mix(filt, product_f)
    gated = (query_f * mixed).astype(jnp.bfloat16)
    grad_mix = jnp.dot(cotangent, proj_weight, preferred_element_type=jnp.float32)
    grad_query = (grad_mix * mixed).astype(jnp.bfloat16)
    grad_gate = (grad_mix * query_f).astype(jnp.bfloat16)
    grad_gate_f = grad_gate.astype(jnp.float32)
    grad_prod = anti_mix(filt, grad_gate_f)
    grad_key = (grad_prod * value_f).astype(jnp.bfloat16)
    grad_value = (grad_prod * key_f).astype(jnp.bfloat16)
    grad_filter = filter_terms(grad_gate_f, product_f)
    grad_proj = lax.dot_general(cotangent, gated, (((0,), (0,)), ((), ())), preferred_element_type=jnp.float32)
    return (grad_query, grad_key, grad_value, grad_filter, grad_proj)
```

```python
import jax
import jax.numpy as jnp
import numpy as np
from jax import lax
from jax.sharding import PartitionSpec as P

TAPS = 128


def from_behind(x, axis, by):
    length = lax.axis_size(axis)
    pairs = [(i, i + by) for i in range(length) if 0 <= i + by < length]
    return lax.ppermute(x, axis, pairs)


def basis(points):
    freqs = points // 2
    phase = (2 * np.arange(freqs)[:, None] + 1) * np.arange(points)[None, :] % (2 * points)
    angle = np.pi * phase / points
    return np.concatenate([np.cos(angle), np.sin(angle)], 0).astype(np.float32)


def split(a):
    a = jnp.asarray(a, jnp.float32)
    hi = a.astype(jnp.bfloat16)
    return hi, (a - hi.astype(jnp.float32)).astype(jnp.bfloat16)


def dot32(a, b):
    return jnp.dot(a, b, preferred_element_type=jnp.float32)


def forward(table, x):
    hi, lo = split(table)
    return dot32(hi, x) + dot32(lo, x)


def backward(table, y):
    thi, tlo = split(table)
    yhi, ylo = split(y)
    return dot32(thi, yhi) + dot32(thi, ylo) + dot32(tlo, yhi)


def halves(x):
    n = x.shape[0] // 2
    return x[:n], x[n:]


def times(x, f):
    (xc, xs), (fc, fs) = halves(x), halves(f)
    return jnp.concatenate([xc * fc - xs * fs, xc * fs + xs * fc], 0)


def times_conj(x, f):
    (xc, xs), (fc, fs) = halves(x), halves(f)
    return jnp.concatenate([xc * fc + xs * fs, xs * fc - xc * fs], 0)


def shards(query_act, key_act, value_act, filters, proj_weight, cotangent):
    tokens = query_act.shape[0]
    points = tokens + TAPS
    table = basis(points)
    inverse = (table.T / (points // 2)).astype(np.float32)
    gathered = lax.all_gather(cotangent, "ch", axis=1, tiled=True)
    weight = lax.all_gather(proj_weight, "ctx", axis=0, tiled=True)
    query_f = query_act.astype(jnp.float32)
    key_f = key_act.astype(jnp.float32)
    value_f = value_act.astype(jnp.float32)
    product = (key_f * value_f).astype(jnp.bfloat16)
    before = from_behind(product[tokens - TAPS :], "ctx", 1)
    filt_spec = forward(table[:, :TAPS], filters.T)
    prod_spec = forward(table[:, :TAPS], before) + forward(table[:, TAPS:], product)
    mixed = backward(inverse[TAPS:], times(prod_spec, filt_spec))
    gated = (query_f * mixed).astype(jnp.bfloat16)
    partial_grad = lax.dot_general(
        gathered, gated, (((0,), (0,)), ((), ())), preferred_element_type=jnp.float32
    ).astype(jnp.bfloat16)
    grad_proj = lax.psum_scatter(partial_grad, "ctx", scatter_dimension=0, tiled=True).astype(
        jnp.float32
    )
    grad_mix = dot32(gathered, weight)
    grad_query = (grad_mix * mixed).astype(jnp.bfloat16)
    grad_gate = (grad_mix * query_f).astype(jnp.bfloat16)
    after = from_behind(grad_gate[:TAPS], "ctx", -1)
    own_spec = forward(table[:, :tokens], grad_gate)
    gate_spec = own_spec + forward(table[:, tokens:], after)
    lags = inverse[TAPS - np.arange(TAPS)]
    local_filter = backward(lags, times_conj(prod_spec, own_spec))
    grad_filter = lax.psum(local_filter, "ctx").T
    grad_prod = backward(inverse[:tokens], times_conj(gate_spec, filt_spec))
    grad_key = (grad_prod * value_f).astype(jnp.bfloat16)
    grad_value = (grad_prod * key_f).astype(jnp.bfloat16)
    return (grad_query, grad_key, grad_value, grad_filter, grad_proj)


def solution(mesh):
    return jax.shard_map(
        shards,
        mesh=mesh,
        in_specs=(
            P("ctx", "ch"),
            P("ctx", "ch"),
            P("ctx", "ch"),
            P("ch", None),
            P("ctx", "ch"),
            P("ctx", "ch"),
        ),
        out_specs=(P("ctx", "ch"), P("ctx", "ch"), P("ctx", "ch"), P("ch", None), P("ctx", "ch")),
        check_vma=False,
    )
```

```python
import functools

import jax
import jax.numpy as jnp
import numpy as np
from jax import lax
from jax.experimental import pallas as pl
from jax.experimental.pallas import tpu as pltpu
from jax.sharding import PartitionSpec as P

TAPS = 128


def from_behind(x, axis, by):
    length = lax.axis_size(axis)
    pairs = [(i, i + by) for i in range(length) if 0 <= i + by < length]
    return lax.ppermute(x, axis, pairs)


def basis(points):
    freqs = points // 2
    phase = (2 * np.arange(freqs)[:, None] + 1) * np.arange(points)[None, :] % (2 * points)
    angle = np.pi * phase / points
    return np.concatenate([np.cos(angle), np.sin(angle)], 0).astype(np.float32)


def split(a):
    a = jnp.asarray(a, jnp.float32)
    hi = a.astype(jnp.bfloat16)
    return hi, (a - hi.astype(jnp.float32)).astype(jnp.bfloat16)


def dot32(a, b):
    return jnp.dot(a, b, preferred_element_type=jnp.float32)


def forward(table, x):
    hi, lo = split(table)
    return dot32(hi, x) + dot32(lo, x)


def backward(table, y):
    thi, tlo = split(table)
    yhi, ylo = split(y)
    return dot32(thi, yhi) + dot32(thi, ylo) + dot32(tlo, yhi)


def halves(x):
    n = x.shape[0] // 2
    return x[:n], x[n:]


def times(x, f):
    (xc, xs), (fc, fs) = halves(x), halves(f)
    return jnp.concatenate([xc * fc - xs * fs, xc * fs + xs * fc], 0)


def times_conj(x, f):
    (xc, xs), (fc, fs) = halves(x), halves(f)
    return jnp.concatenate([xc * fc + xs * fs, xs * fc - xc * fs], 0)


MESH = pl.DeviceIdType.MESH
CHUNKS = 4


def exchange_kernel(n_ctx, n_ch, cot, weight, gated, grad_mix, grad_proj, blocks, weights, mine,
                    partner_out, partner_in, arrived, own_sem, z_send, z_recv, w_send, w_recv,
                    f_send, f_recv, p_send, p_recv, r_send, r_recv):
    chips = n_ctx // 2
    per = n_ctx // n_ch
    hops = n_ch - 1
    ctx = lax.axis_index("ctx")
    ch = lax.axis_index("ch")
    chip, core = ctx // 2, ctx % 2
    other = chip * 2 + 1 - core
    rows = weight.shape[0]
    wide = rows // CHUNKS

    def chip_at(off):
        return (chip + off) % chips

    barrier = pltpu.get_barrier_semaphore()
    for off in range(1, n_ctx):
        pl.semaphore_signal(barrier, inc=1, device_id=((ctx + off) % n_ctx, ch), device_id_type=MESH)
    for off in (1, n_ch - 1):
        pl.semaphore_signal(barrier, inc=1, device_id=(ctx, (ch + off) % n_ch), device_id_type=MESH)

    def own_copy(s, e):
        return pltpu.make_async_copy(
            cot.at[:, pl.ds(e * rows + s * wide, wide)], blocks.at[ch, s, e], own_sem.at[s, e]
        )

    own_weight = pltpu.make_async_copy(weight, weights.at[ctx], own_sem.at[CHUNKS, 0])
    for s in range(CHUNKS):
        for e in range(per):
            own_copy(s, e).start()
    own_weight.start()
    pl.semaphore_wait(barrier, n_ctx + 1)

    def w_copy(off):
        return pltpu.make_async_remote_copy(
            weight, weights.at[ctx], w_send.at[off], w_recv.at[off],
            device_id=(chip_at(off) * 2 + core, ch), device_id_type=MESH)

    def f_copy(off):
        owner = chip_at(chips - off) * 2 + core
        return pltpu.make_async_remote_copy(
            weights.at[owner], weights.at[owner], f_send.at[off], f_recv.at[off],
            device_id=(other, ch), device_id_type=MESH)

    def z_copy(s, h, way):
        if way == 0:
            block, to = ch - h, ch + 1
        else:
            block, to = ch + h, ch - 1
        block = jnp.clip(block, 0, n_ch - 1)
        return pltpu.make_async_remote_copy(
            blocks.at[block, s], blocks.at[block, s], z_send.at[s, h, way], z_recv.at[s, h, way],
            device_id=(ctx, jnp.clip(to, 0, n_ch - 1)), device_id_type=MESH)

    def sends(h, way):
        if way == 0:
            return jnp.logical_and(ch >= h, ch < n_ch - 1)
        return jnp.logical_and(ch + h < n_ch, ch > 0)

    def receives(h, way):
        if way == 0:
            return ch - 1 - h >= 0
        return ch + 1 + h < n_ch

    def p_copy(s, k):
        return pltpu.make_async_remote_copy(
            partner_out.at[s % 2, k], partner_in.at[s, k], p_send.at[s, k], p_recv.at[s, k],
            device_id=(other, ch), device_id_type=MESH)

    def r_copy(s, off):
        return pltpu.make_async_remote_copy(
            partner_in.at[s, chip_at(off)], arrived.at[s, off], r_send.at[s, off],
            r_recv.at[s, off], device_id=(chip_at(off) * 2 + core, ch), device_id_type=MESH)

    def partial_sum(s, k, e):
        target = k * 2 + e
        return lax.dot_general(
            blocks[target // per, s, target % per], gated[...], (((0,), (0,)), ((), ())),
            preferred_element_type=jnp.float32)

    def reduce_chunk(s):
        @pl.loop(0, chips)
        def _(k):
            if s >= 2:
                p_copy(s - 2, k).wait_send()
            partner_out[s % 2, k] = partial_sum(s, k, 1 - core).astype(jnp.bfloat16)
            p_copy(s, k).start()

        @pl.loop(0, chips)
        def _(k):
            mine[k] = partial_sum(s, k, core)

        @pl.loop(1, chips)
        def _(off):
            k = chip_at(off)
            p_copy(s, k).wait_recv()
            partner_in[s, k] = (mine[k] + partner_in[s, k].astype(jnp.float32)).astype(jnp.bfloat16)
            r_copy(s, off).start()

        p_copy(s, chip).wait_recv()
        grad_proj[pl.ds(s * wide, wide), :] = mine[chip] + partner_in[s, chip].astype(jnp.float32)

    def finish_chunk(s):
        @pl.loop(1, chips)
        def _(off):
            r_copy(s, off).wait_recv()
            grad_proj[pl.ds(s * wide, wide), :] += arrived[s, off].astype(jnp.float32)

    for stage in range(CHUNKS + hops - 1):
        if stage < CHUNKS:
            for e in range(per):
                own_copy(stage, e).wait()
        for h in reversed(range(hops)):
            s = stage - h
            if 0 <= s < CHUNKS:
                for way in range(2):
                    @pl.when(sends(h, way))
                    def _():
                        z_copy(s, h, way).start()
        if stage == 0:
            @pl.loop(1, chips)
            def _(off):
                w_copy(off).start()
            own_weight.wait()
            f_copy(0).start()
        if stage >= hops:
            reduce_chunk(stage - hops)
        for h in range(hops):
            s = stage - h
            if 0 <= s < CHUNKS:
                for way in range(2):
                    @pl.when(receives(h, way))
                    def _():
                        z_copy(s, h, way).wait_recv()
        if stage == hops - 1:
            @pl.loop(1, chips)
            def _(off):
                w_copy(off).wait_recv()
                f_copy(off).start()
    reduce_chunk(CHUNKS - 1)

    @pl.loop(0, chips)
    def _(off):
        f_copy(off).wait_recv()

    grad_mix[...] = jnp.zeros_like(grad_mix)

    @pl.loop(0, n_ctx)
    def _(i):
        total = grad_mix[...]
        for s in range(CHUNKS):
            total += jnp.dot(
                blocks[i // per, s, i % per], weights[i, pl.ds(s * wide, wide), :],
                preferred_element_type=jnp.float32)
        grad_mix[...] = total

    for s in range(CHUNKS):
        finish_chunk(s)

    for s in range(CHUNKS):
        for h in range(hops):
            for way in range(2):
                @pl.when(sends(h, way))
                def _():
                    z_copy(s, h, way).wait_send()

        @pl.loop(1, chips)
        def _(off):
            r_copy(s, off).wait_send()

        if s >= CHUNKS - 2:
            @pl.loop(0, chips)
            def _(k):
                p_copy(s, k).wait_send()

    @pl.loop(1, chips)
    def _(off):
        w_copy(off).wait_send()

    @pl.loop(0, chips)
    def _(off):
        f_copy(off).wait_send()


def exchange(cotangent, proj_weight, gated):
    n_ctx, n_ch = lax.axis_size("ctx"), lax.axis_size("ch")
    tokens, channels = gated.shape
    rows = proj_weight.shape[0]
    wide = rows // CHUNKS
    chips, per, hops = n_ctx // 2, n_ctx // n_ch, n_ch - 1
    dma = pltpu.SemaphoreType.DMA
    return pl.pallas_call(
        functools.partial(exchange_kernel, n_ctx, n_ch),
        out_shape=(
            jax.ShapeDtypeStruct((tokens, channels), jnp.float32),
            jax.ShapeDtypeStruct((rows, channels), jnp.float32),
        ),
        in_specs=[
            pl.BlockSpec(memory_space=pl.ANY),
            pl.BlockSpec(memory_space=pl.ANY),
            pl.BlockSpec(memory_space=pltpu.VMEM),
        ],
        out_specs=[pl.BlockSpec(memory_space=pltpu.VMEM)] * 2,
        scratch_shapes=[
            pltpu.VMEM((n_ch, CHUNKS, per, tokens, wide), jnp.bfloat16),
            pltpu.VMEM((n_ctx, rows, channels), jnp.bfloat16),
            pltpu.VMEM((chips, wide, channels), jnp.float32),
            pltpu.VMEM((2, chips, wide, channels), jnp.bfloat16),
            pltpu.VMEM((CHUNKS, chips, wide, channels), jnp.bfloat16),
            pltpu.VMEM((CHUNKS, chips, wide, channels), jnp.bfloat16),
            dma((CHUNKS + 1, per)),
            dma((CHUNKS, hops, 2)),
            dma((CHUNKS, hops, 2)),
            dma((chips,)),
            dma((chips,)),
            dma((chips,)),
            dma((chips,)),
            dma((CHUNKS, chips)),
            dma((CHUNKS, chips)),
            dma((CHUNKS, chips)),
            dma((CHUNKS, chips)),
        ],
        compiler_params=pltpu.CompilerParams(
            collective_id=0, has_side_effects=True, vmem_limit_bytes=62 * 2**20
        ),
    )(cotangent, proj_weight, gated)


def shards(query_act, key_act, value_act, filters, proj_weight, cotangent):
    tokens = query_act.shape[0]
    points = tokens + TAPS
    table = basis(points)
    inverse = (table.T / (points // 2)).astype(np.float32)
    query_f = query_act.astype(jnp.float32)
    key_f = key_act.astype(jnp.float32)
    value_f = value_act.astype(jnp.float32)
    product = (key_f * value_f).astype(jnp.bfloat16)
    before = from_behind(product[tokens - TAPS :], "ctx", 1)
    filt_spec = forward(table[:, :TAPS], filters.T)
    prod_spec = forward(table[:, :TAPS], before) + forward(table[:, TAPS:], product)
    mixed = backward(inverse[TAPS:], times(prod_spec, filt_spec))
    gated = (query_f * mixed).astype(jnp.bfloat16)
    grad_mix, grad_proj = exchange(cotangent, proj_weight, gated)
    grad_query = (grad_mix * mixed).astype(jnp.bfloat16)
    grad_gate = (grad_mix * query_f).astype(jnp.bfloat16)
    after = from_behind(grad_gate[:TAPS], "ctx", -1)
    own_spec = forward(table[:, :tokens], grad_gate)
    gate_spec = own_spec + forward(table[:, tokens:], after)
    lags = inverse[TAPS - np.arange(TAPS)]
    local_filter = backward(lags, times_conj(prod_spec, own_spec))
    grad_filter = lax.psum(local_filter, "ctx").T
    grad_prod = backward(inverse[:tokens], times_conj(gate_spec, filt_spec))
    grad_key = (grad_prod * value_f).astype(jnp.bfloat16)
    grad_value = (grad_prod * key_f).astype(jnp.bfloat16)
    return (grad_query, grad_key, grad_value, grad_filter, grad_proj)


def solution(mesh):
    return jax.shard_map(
        shards,
        mesh=mesh,
        in_specs=(
            P("ctx", "ch"),
            P("ctx", "ch"),
            P("ctx", "ch"),
            P("ch", None),
            P("ctx", "ch"),
            P("ctx", "ch"),
        ),
        out_specs=(P("ctx", "ch"), P("ctx", "ch"), P("ctx", "ch"), P("ch", None), P("ctx", "ch")),
        check_vma=False,
    )
```

```python
import functools

import jax
import jax.numpy as jnp
import numpy as np
from jax import lax
from jax.experimental import pallas as pl
from jax.experimental.pallas import tpu as pltpu
from jax.sharding import PartitionSpec as P

TAPS = 128


def from_behind(x, axis, by):
    length = lax.axis_size(axis)
    pairs = [(i, i + by) for i in range(length) if 0 <= i + by < length]
    return lax.ppermute(x, axis, pairs)


def basis(points):
    freqs = points // 2
    phase = (2 * np.arange(freqs)[:, None] + 1) * np.arange(points)[None, :] % (2 * points)
    angle = np.pi * phase / points
    return np.concatenate([np.cos(angle), np.sin(angle)], 0).astype(np.float32)


def split(a):
    a = jnp.asarray(a, jnp.float32)
    hi = a.astype(jnp.bfloat16)
    return hi, (a - hi.astype(jnp.float32)).astype(jnp.bfloat16)


def dot32(a, b):
    return jnp.dot(a, b, preferred_element_type=jnp.float32)


def forward(table, x):
    hi, lo = split(table)
    return dot32(hi, x) + dot32(lo, x)


def backward(table, y):
    thi, tlo = split(table)
    yhi, ylo = split(y)
    return dot32(thi, yhi) + dot32(thi, ylo) + dot32(tlo, yhi)


def halves(x):
    n = x.shape[0] // 2
    return x[:n], x[n:]


def times(x, f):
    (xc, xs), (fc, fs) = halves(x), halves(f)
    return jnp.concatenate([xc * fc - xs * fs, xc * fs + xs * fc], 0)


def times_conj(x, f):
    (xc, xs), (fc, fs) = halves(x), halves(f)
    return jnp.concatenate([xc * fc + xs * fs, xs * fc - xc * fs], 0)


MESH = pl.DeviceIdType.MESH
CHUNKS = 4


def exchange_kernel(n_ctx, n_ch, cot, weight, gated, query, grad_mix, gate, after, grad_proj, blocks, weights, mine,
                    partner_out, partner_in, arrived, own_sem, z_send, z_recv, w_send, w_recv,
                    f_send, f_recv, p_send, p_recv, r_send, r_recv, h_sem):
    chips = n_ctx // 2
    per = n_ctx // n_ch
    hops = n_ch - 1
    ctx = lax.axis_index("ctx")
    ch = lax.axis_index("ch")
    chip, core = ctx // 2, ctx % 2
    other = chip * 2 + 1 - core
    rows = weight.shape[0]
    wide = rows // CHUNKS

    def chip_at(off):
        return (chip + off) % chips

    barrier = pltpu.get_barrier_semaphore()
    for off in range(1, n_ctx):
        pl.semaphore_signal(barrier, inc=1, device_id=((ctx + off) % n_ctx, ch), device_id_type=MESH)
    for off in (1, n_ch - 1):
        pl.semaphore_signal(barrier, inc=1, device_id=(ctx, (ch + off) % n_ch), device_id_type=MESH)

    def own_copy(s, e):
        return pltpu.make_async_copy(
            cot.at[:, pl.ds(e * rows + s * wide, wide)], blocks.at[ch, s, e], own_sem.at[s, e]
        )

    own_weight = pltpu.make_async_copy(weight, weights.at[ctx], own_sem.at[CHUNKS, 0])
    for s in range(CHUNKS):
        for e in range(per):
            own_copy(s, e).start()
    own_weight.start()
    pl.semaphore_wait(barrier, n_ctx + 1)

    def w_copy(off):
        return pltpu.make_async_remote_copy(
            weight, weights.at[ctx], w_send.at[off], w_recv.at[off],
            device_id=(chip_at(off) * 2 + core, ch), device_id_type=MESH)

    def f_copy(off):
        owner = chip_at(chips - off) * 2 + core
        return pltpu.make_async_remote_copy(
            weights.at[owner], weights.at[owner], f_send.at[off], f_recv.at[off],
            device_id=(other, ch), device_id_type=MESH)

    def z_copy(s, h, way):
        if way == 0:
            block, to = ch - h, ch + 1
        else:
            block, to = ch + h, ch - 1
        block = jnp.clip(block, 0, n_ch - 1)
        return pltpu.make_async_remote_copy(
            blocks.at[block, s], blocks.at[block, s], z_send.at[s, h, way], z_recv.at[s, h, way],
            device_id=(ctx, jnp.clip(to, 0, n_ch - 1)), device_id_type=MESH)

    def sends(h, way):
        if way == 0:
            return jnp.logical_and(ch >= h, ch < n_ch - 1)
        return jnp.logical_and(ch + h < n_ch, ch > 0)

    def receives(h, way):
        if way == 0:
            return ch - 1 - h >= 0
        return ch + 1 + h < n_ch

    def p_copy(s, k):
        return pltpu.make_async_remote_copy(
            partner_out.at[s % 2, k], partner_in.at[s, k], p_send.at[s, k], p_recv.at[s, k],
            device_id=(other, ch), device_id_type=MESH)

    def r_copy(s, off):
        return pltpu.make_async_remote_copy(
            partner_in.at[s, chip_at(off)], arrived.at[s, off - 1], r_send.at[s, off],
            r_recv.at[s, off], device_id=(chip_at(off) * 2 + core, ch), device_id_type=MESH)

    halo_copy = pltpu.make_async_remote_copy(
        gate.at[pl.ds(0, TAPS)], after, h_sem.at[0], h_sem.at[1],
        device_id=(jnp.maximum(ctx - 1, 0), ch), device_id_type=MESH)

    def mix_chunk(s):
        if s == 0:
            @pl.loop(0, chips)
            def _(off):
                f_copy(off).wait_recv()

            grad_mix[...] = jnp.zeros_like(grad_mix)

        @pl.loop(0, n_ctx)
        def _(i):
            grad_mix[...] += jnp.dot(
                blocks[i // per, s, i % per], weights[i, pl.ds(s * wide, wide), :],
                preferred_element_type=jnp.float32)

    def partial_sum(s, k, e):
        target = k * 2 + e
        return lax.dot_general(
            blocks[target // per, s, target % per], gated[...], (((0,), (0,)), ((), ())),
            preferred_element_type=jnp.float32)

    def reduce_chunk(s):
        @pl.loop(0, chips)
        def _(k):
            if s >= 2:
                p_copy(s - 2, k).wait_send()
            partner_out[s % 2, k] = partial_sum(s, k, 1 - core).astype(jnp.bfloat16)
            p_copy(s, k).start()

        @pl.loop(0, chips)
        def _(k):
            mine[k] = partial_sum(s, k, core)

        @pl.loop(1, chips)
        def _(off):
            k = chip_at(off)
            p_copy(s, k).wait_recv()
            partner_in[s, k] = (mine[k] + partner_in[s, k].astype(jnp.float32)).astype(jnp.bfloat16)
            r_copy(s, off).start()

        p_copy(s, chip).wait_recv()
        grad_proj[pl.ds(s * wide, wide), :] = mine[chip] + partner_in[s, chip].astype(jnp.float32)

    def finish_chunk(s):
        @pl.loop(1, chips)
        def _(off):
            r_copy(s, off).wait_recv()
            grad_proj[pl.ds(s * wide, wide), :] += arrived[s, off - 1].astype(jnp.float32)

    for stage in range(CHUNKS + hops - 1):
        fresh = [s for s in ((0, 1) if stage == 0 else (stage + 1,)) if s < CHUNKS]
        for s in fresh:
            for e in range(per):
                own_copy(s, e).wait()
        ready = [(stage - h, h) for h in reversed(range(1, hops))] + [(s, 0) for s in fresh]
        for s, h in ready:
            if 0 <= s < CHUNKS:
                for way in range(2):
                    @pl.when(sends(h, way))
                    def _():
                        z_copy(s, h, way).start()
        if stage == 0:
            @pl.loop(1, chips)
            def _(off):
                w_copy(off).start()
            own_weight.wait()
            f_copy(0).start()
        if stage >= hops:
            reduce_chunk(stage - hops)
        if hops < stage < CHUNKS + hops - 2:
            mix_chunk(stage - hops - 1)
        for h in range(hops):
            s = stage - h
            if 0 <= s < CHUNKS:
                for way in range(2):
                    @pl.when(receives(h, way))
                    def _():
                        z_copy(s, h, way).wait_recv()
        if stage == hops - 1:
            @pl.loop(1, chips)
            def _(off):
                w_copy(off).wait_recv()
                f_copy(off).start()
    reduce_chunk(CHUNKS - 1)

    for s in range(CHUNKS - 3, CHUNKS):
        mix_chunk(s)
    gate[...] = (grad_mix[...] * query[...].astype(jnp.float32)).astype(jnp.bfloat16)

    @pl.when(ctx > 0)
    def _():
        halo_copy.start()

    @pl.when(ctx == n_ctx - 1)
    def _():
        after[...] = jnp.zeros_like(after)

    for s in range(CHUNKS):
        finish_chunk(s)

    for s in range(CHUNKS):
        for h in range(hops):
            for way in range(2):
                @pl.when(sends(h, way))
                def _():
                    z_copy(s, h, way).wait_send()

        @pl.loop(1, chips)
        def _(off):
            r_copy(s, off).wait_send()

        if s >= CHUNKS - 2:
            @pl.loop(0, chips)
            def _(k):
                p_copy(s, k).wait_send()

    @pl.when(ctx > 0)
    def _():
        halo_copy.wait_send()

    @pl.when(ctx < n_ctx - 1)
    def _():
        halo_copy.wait_recv()

    @pl.loop(1, chips)
    def _(off):
        w_copy(off).wait_send()

    @pl.loop(0, chips)
    def _(off):
        f_copy(off).wait_send()


def exchange(cotangent, proj_weight, gated, query_act):
    n_ctx, n_ch = lax.axis_size("ctx"), lax.axis_size("ch")
    tokens, channels = gated.shape
    rows = proj_weight.shape[0]
    wide = rows // CHUNKS
    chips, per, hops = n_ctx // 2, n_ctx // n_ch, n_ch - 1
    dma = pltpu.SemaphoreType.DMA
    return pl.pallas_call(
        functools.partial(exchange_kernel, n_ctx, n_ch),
        out_shape=(
            jax.ShapeDtypeStruct((tokens, channels), jnp.float32),
            jax.ShapeDtypeStruct((tokens, channels), jnp.bfloat16),
            jax.ShapeDtypeStruct((TAPS, channels), jnp.bfloat16),
            jax.ShapeDtypeStruct((rows, channels), jnp.float32),
        ),
        in_specs=[
            pl.BlockSpec(memory_space=pl.ANY),
            pl.BlockSpec(memory_space=pl.ANY),
            pl.BlockSpec(memory_space=pltpu.VMEM),
            pl.BlockSpec(memory_space=pltpu.VMEM),
        ],
        out_specs=[pl.BlockSpec(memory_space=pltpu.VMEM)] * 4,
        scratch_shapes=[
            pltpu.VMEM((n_ch, CHUNKS, per, tokens, wide), jnp.bfloat16),
            pltpu.VMEM((n_ctx, rows, channels), jnp.bfloat16),
            pltpu.VMEM((chips, wide, channels), jnp.float32),
            pltpu.VMEM((2, chips, wide, channels), jnp.bfloat16),
            pltpu.VMEM((CHUNKS, chips, wide, channels), jnp.bfloat16),
            pltpu.VMEM((CHUNKS, chips - 1, wide, channels), jnp.bfloat16),
            dma((CHUNKS + 1, per)),
            dma((CHUNKS, hops, 2)),
            dma((CHUNKS, hops, 2)),
            dma((chips,)),
            dma((chips,)),
            dma((chips,)),
            dma((chips,)),
            dma((CHUNKS, chips)),
            dma((CHUNKS, chips)),
            dma((CHUNKS, chips)),
            dma((CHUNKS, chips)),
            dma((2,)),
        ],
        compiler_params=pltpu.CompilerParams(
            collective_id=0, has_side_effects=True, vmem_limit_bytes=62 * 2**20
        ),
    )(cotangent, proj_weight, gated, query_act)


def sum_kernel(n_ctx, x, out, arrived, r_send, r_recv, g_send, g_recv):
    ctx = lax.axis_index("ctx")
    ch = lax.axis_index("ch")
    share = x.shape[0] // n_ctx
    barrier = pltpu.get_barrier_semaphore()

    def peer(off):
        return (ctx + off) % n_ctx

    def piece(i):
        return pl.ds(pl.multiple_of(i * share, share), share)

    @pl.loop(1, n_ctx)
    def _(off):
        pl.semaphore_signal(barrier, inc=1, device_id=(peer(off), ch), device_id_type=MESH)

    pl.semaphore_wait(barrier, n_ctx - 1)

    def scatter(off):
        return pltpu.make_async_remote_copy(
            x.at[piece(peer(off))], arrived.at[off - 1], r_send.at[off - 1], r_recv.at[off - 1],
            device_id=(peer(off), ch), device_id_type=MESH)

    def gather(off):
        return pltpu.make_async_remote_copy(
            out.at[piece(ctx)], out.at[piece(ctx)], g_send.at[off - 1], g_recv.at[off - 1],
            device_id=(peer(off), ch), device_id_type=MESH)

    def gathered(off):
        source = piece(peer(n_ctx - off))
        return pltpu.make_async_remote_copy(
            out.at[source], out.at[source], g_send.at[off - 1], g_recv.at[off - 1],
            device_id=(peer(off), ch), device_id_type=MESH)

    @pl.loop(1, n_ctx)
    def _(off):
        scatter(off).start()

    total = x[piece(ctx), :]
    for off in range(1, n_ctx):
        scatter(off).wait_recv()
        total += arrived[off - 1]
    out[piece(ctx), :] = total

    @pl.loop(1, n_ctx)
    def _(off):
        gather(off).start()

    @pl.loop(1, n_ctx)
    def _(off):
        gathered(off).wait_recv()
        gather(off).wait_send()
        scatter(off).wait_send()


def summed_over_tokens(x):
    n_ctx = lax.axis_size("ctx")
    dma = pltpu.SemaphoreType.DMA
    return pl.pallas_call(
        functools.partial(sum_kernel, n_ctx),
        out_shape=jax.ShapeDtypeStruct(x.shape, x.dtype),
        in_specs=[pl.BlockSpec(memory_space=pltpu.VMEM)],
        out_specs=pl.BlockSpec(memory_space=pltpu.VMEM),
        scratch_shapes=[pltpu.VMEM((n_ctx - 1, x.shape[0] // n_ctx, x.shape[1]), x.dtype)]
        + [dma((n_ctx - 1,))] * 4,
        compiler_params=pltpu.CompilerParams(collective_id=1, has_side_effects=True),
    )(x)


def shards(query_act, key_act, value_act, filters, proj_weight, cotangent):
    tokens = query_act.shape[0]
    points = tokens + TAPS
    table = basis(points)
    inverse = (table.T / (points // 2)).astype(np.float32)
    query_f = query_act.astype(jnp.float32)
    key_f = key_act.astype(jnp.float32)
    value_f = value_act.astype(jnp.float32)
    product = (key_f * value_f).astype(jnp.bfloat16)
    before = from_behind(product[tokens - TAPS :], "ctx", 1)
    filt_spec = forward(table[:, :TAPS], filters.T)
    prod_spec = forward(table[:, :TAPS], before) + forward(table[:, TAPS:], product)
    mixed = backward(inverse[TAPS:], times(prod_spec, filt_spec))
    gated = (query_f * mixed).astype(jnp.bfloat16)
    grad_mix, grad_gate, after, grad_proj = exchange(cotangent, proj_weight, gated, query_act)
    grad_query = (grad_mix * mixed).astype(jnp.bfloat16)
    own_spec = forward(table[:, :tokens], grad_gate)
    gate_spec = own_spec + forward(table[:, tokens:], after)
    lags = inverse[TAPS - np.arange(TAPS)]
    local_filter = backward(lags, times_conj(prod_spec, own_spec))
    grad_filter = summed_over_tokens(local_filter).T
    grad_prod = backward(inverse[:tokens], times_conj(gate_spec, filt_spec))
    grad_key = (grad_prod * value_f).astype(jnp.bfloat16)
    grad_value = (grad_prod * key_f).astype(jnp.bfloat16)
    return (grad_query, grad_key, grad_value, grad_filter, grad_proj)


def solution(mesh):
    return jax.shard_map(
        shards,
        mesh=mesh,
        in_specs=(
            P("ctx", "ch"),
            P("ctx", "ch"),
            P("ctx", "ch"),
            P("ch", None),
            P("ctx", "ch"),
            P("ctx", "ch"),
        ),
        out_specs=(P("ctx", "ch"), P("ctx", "ch"), P("ctx", "ch"), P("ch", None), P("ctx", "ch")),
        check_vma=False,
    )
```
